32 devices in a mesh: patch: 8 (over y, x, core), tensor: 2 (over z_hi), guide: 2 (over z_lo).
Axes of the slice: x: 2, y: 2, z: 4 (z_hi: 2, z_lo: 2; z = z_hi * 2 + z_lo), core: 2. Of those that a mesh axis runs over, the one named last changes fastest.
Arguments:
- fresh_q: bfloat16 [2, 1536, 2560], P('guide', 'patch', 'tensor'), may hold values from -61 to 61
- fresh_k: bfloat16 [2, 1536, 2560], P('guide', 'patch', 'tensor'), may hold values from -45 to 45
- fresh_v: bfloat16 [2, 1536, 2560], P('guide', 'patch', 'tensor'), may hold values from -6 to 6
- stale_k: bfloat16 [2, 1536, 2560], P('guide', 'patch', 'tensor'), may hold values from -45 to 45
- stale_v: bfloat16 [2, 1536, 2560], P('guide', 'patch', 'tensor'), may hold values from -6 to 6
- positions: int32 [3, 1536], P(None, 'patch'), may hold values from 0 to 31
- residual: bfloat16 [2, 1536, 5120], P('guide', 'patch', 'tensor'), may hold values from -3 to 3
- out_weight: bfloat16 [2560, 5120], P('tensor'), may hold values from -0.125 to 0.125
- gate_table: float32 [50, 5120], replicated, may hold values from 0.3 to 3
- timestep: int32 [1], replicated, may hold values from 0 to 49
Outputs:
- guided: bfloat16 [1536, 5120], P('patch', ('tensor', 'guide'))
The draws below stay inside these ranges and needn't reach their ends.
All inputs are finite; a program needn't handle non-finite values.
Results may differ from the reference program's by a relative error of at most 0.011.
Values may be sent and summed in bfloat16 or wider, within the bound.
No kernel may reach another device: no remote copies, remote signals or barrier semaphores. Data moves between devices by JAX's collectives and lax.ppermute only.
A program may use at most 128 MiB of HBM per device.

```python
import math
import jax
import jax.numpy as jnp
from jax import lax

D = 5120
HEADS = 20
HEAD_DIM = 128
STEPS = 50
GRID = 32
TOK_DEV = 192
TOKENS = 1536
HD = 2560
N_PATCH = 8


def key_entries(key, salt):
    base_key = jax.random.fold_in(key, salt)
    entries = jnp.clip(2.5 * jax.random.normal(base_key, (2, TOKENS, HEADS, HEAD_DIM), jnp.float32), -12.0, 12.0)
    return entries.reshape(2, TOKENS, HEADS * HEAD_DIM)


def draw_fresh_k(key, part):
    return key_entries(key, 17).astype(jnp.bfloat16)


def draw_stale_k(key, part):
    return key_entries(key, 19).astype(jnp.bfloat16)


def draw_fresh_q(key, part):
    base_key = jax.random.fold_in(key, 13)
    entries = jnp.clip(jax.random.normal(base_key, (2, TOKENS, HEADS, HEAD_DIM), jnp.float32), -6.0, 6.0)
    return entries.reshape(2, TOKENS, HEADS * HEAD_DIM).astype(jnp.bfloat16)


def with_ends(values, rng, smallest, top_value):
    dims = values.shape
    spot = [jax.random.randint(jax.random.fold_in(rng, axis), (), 0, dims[axis]) for axis in range(len(dims))]
    values = values.at[tuple(spot)].set(smallest)
    longest = dims.index(max(dims))
    spot[longest] = (spot[longest] + 1) % dims[longest]
    return values.at[tuple(spot)].set(top_value)


def block_levels(own_key, dims, cuts, least, high):
    def one(axis_at, parts):
        heights = jax.random.uniform(jax.random.fold_in(jax.random.fold_in(own_key, 6), axis_at), (parts,), jnp.float32, least / len(cuts), high / len(cuts))
        return jnp.repeat(jnp.exp(heights), dims[axis_at] // parts).reshape((-1,) + (1,) * (len(dims) - axis_at - 1))

    gain = one(*cuts[0])
    for cut in cuts[1:]:
        gain = gain * one(*cut)
    return gain


def bell_draw(own_key, shape, deviation, reach, pieces=(), kind=jnp.bfloat16):
    drawn = jax.random.normal(own_key, shape, jnp.float32) * deviation
    if len(pieces) > 0:
        drawn = block_levels(own_key, shape, pieces, -0.22, 0.18) * drawn
    return jnp.clip(drawn, min=-reach, max=reach).astype(kind)


def setup_inputs(seed: int = 0) -> dict:
    key_list = jax.random.split(jax.random.key(seed), 11)
    return {
        "fresh_q": draw_fresh_q(jax.random.fold_in(key_list[10], 71), 0),
        "fresh_k": draw_fresh_k(jax.random.fold_in(key_list[10], 71), 0),
        "fresh_v": bell_draw(key_list[2], (2, TOKENS, HD), 1.0, 6.0, ((0, 2), (1, 8), (2, 2))),
        "stale_k": draw_stale_k(jax.random.fold_in(key_list[10], 71), 0),
        "stale_v": bell_draw(key_list[4], (2, TOKENS, HD), 1.0, 6.0, ((0, 2), (1, 8), (2, 2))),
        "positions": with_ends(jax.random.randint(key_list[5], (3, TOKENS), 0, GRID), jax.random.fold_in(key_list[5], 1), 0, GRID - 1).astype(jnp.int32),
        "residual": bell_draw(key_list[6], (2, TOKENS, D), 0.5, 3.0, ((0, 2), (1, 8), (2, 2))),
        "out_weight": bell_draw(key_list[7], (HD, D), HD ** -0.5, 0.125, ((0, 2),)),
        "gate_table": jnp.clip(jnp.exp(jax.random.uniform(key_list[8], (STEPS, D), jnp.float32, math.log(0.3), math.log(3.0))), 0.3, 3.0),
        "timestep": jax.random.randint(key_list[9], (1,), 0, STEPS).astype(jnp.int32),
    }


def rotate_positions(values, positions):
    rows_count = values.shape[0]
    width = values.shape[1]
    head_count = width // HEAD_DIM
    half_dim = HEAD_DIM // 2
    side_pairs = HEAD_DIM // 6
    frame_pairs = half_dim - 2 * side_pairs
    pair_index = lax.iota(jnp.int32, half_dim)
    section = (pair_index >= frame_pairs).astype(jnp.int32) + (pair_index >= frame_pairs + side_pairs).astype(jnp.int32)
    local_index = pair_index - jnp.where(section == 0, 0, jnp.where(section == 1, frame_pairs, frame_pairs + side_pairs))
    section_pairs = jnp.where(section == 0, frame_pairs, side_pairs)
    exponent = local_index.astype(jnp.float32) / section_pairs.astype(jnp.float32)
    freqs = jnp.power(jnp.float32(10000.0), -exponent)
    place = positions.astype(jnp.float32)
    chosen = jnp.where(section[None, :] == 0, place[0][:, None], jnp.where(section[None, :] == 1, place[1][:, None], place[2][:, None]))
    angles = chosen * freqs[None, :]
    cosines = jnp.repeat(jnp.cos(angles), 2, axis=1)
    sines = jnp.repeat(jnp.sin(angles), 2, axis=1)
    row_ids = lax.iota(jnp.int32, HEAD_DIM)[:, None]
    col_ids = lax.iota(jnp.int32, HEAD_DIM)[None, :]
    swap_table = jnp.where((row_ids % 2 == 1) & (col_ids == row_ids - 1), -1.0, jnp.where((row_ids % 2 == 0) & (col_ids == row_ids + 1), 1.0, 0.0)).astype(jnp.float32)
    shaped = values.astype(jnp.float32).reshape(rows_count, head_count, HEAD_DIM)
    turned = jnp.einsum('thd,de->the', shaped, swap_table, precision=lax.Precision.HIGHEST)
    result = shaped * cosines[:, None, :] + turned * sines[:, None, :]
    return result.reshape(rows_count, width)

def reference(fresh_q, fresh_k, fresh_v, stale_k, stale_v, positions, residual, out_weight, gate_table, timestep):
    queries = jnp.stack([rotate_positions(fresh_q[0], positions), rotate_positions(fresh_q[1], positions)]).astype(jnp.bfloat16)
    new_keys = jnp.stack([rotate_positions(fresh_k[0], positions), rotate_positions(fresh_k[1], positions)]).astype(jnp.bfloat16)
    queries = lax.optimization_barrier(queries)
    new_keys = lax.optimization_barrier(new_keys)
    score_scale = 1.0 / math.sqrt(HEAD_DIM)

    def attend_block(index):
        branch = index // N_PATCH
        block = index % N_PATCH
        start = (block * TOK_DEV).astype(jnp.int32)
        branch_q = lax.dynamic_index_in_dim(queries, branch, 0, keepdims=False)
        branch_k = lax.dynamic_index_in_dim(new_keys, branch, 0, keepdims=False)
        branch_v = lax.dynamic_index_in_dim(fresh_v, branch, 0, keepdims=False)
        old_k = lax.dynamic_index_in_dim(stale_k, branch, 0, keepdims=False)
        old_v = lax.dynamic_index_in_dim(stale_v, branch, 0, keepdims=False)
        query_rows = lax.dynamic_slice_in_dim(branch_q, start, TOK_DEV, 0)
        key_rows = lax.dynamic_update_slice_in_dim(old_k, lax.dynamic_slice_in_dim(branch_k, start, TOK_DEV, 0), start, 0)
        value_rows = lax.dynamic_update_slice_in_dim(old_v, lax.dynamic_slice_in_dim(branch_v, start, TOK_DEV, 0), start, 0)
        q_heads = query_rows.astype(jnp.float32).reshape(TOK_DEV, HEADS, HEAD_DIM)
        k_heads = key_rows.astype(jnp.float32).reshape(TOKENS, HEADS, HEAD_DIM)
        v_heads = value_rows.astype(jnp.float32).reshape(TOKENS, HEADS, HEAD_DIM)
        scores = jnp.einsum('qhd,khd->hqk', q_heads, k_heads) * score_scale
        top_score = lax.optimization_barrier(jnp.max(scores, axis=2, keepdims=True))
        expo = jnp.exp(scores - top_score)
        total = lax.optimization_barrier(jnp.sum(expo, axis=2))
        weights = lax.optimization_barrier(expo.astype(jnp.bfloat16)).astype(jnp.float32)
        summed = jnp.einsum('hqk,khd->qhd', weights, v_heads)
        result = summed / jnp.transpose(total)[:, :, None]
        return result.reshape(TOK_DEV, HD).astype(jnp.bfloat16)
    blocks = lax.map(attend_block, jnp.arange(2 * N_PATCH, dtype=jnp.int32))
    attn = blocks.reshape(2, TOKENS, HD)
    one_hot = (lax.iota(jnp.int32, STEPS) == timestep[0]).astype(jnp.float32)[None, :]
    gate_row = jnp.dot(one_hot, gate_table, precision=lax.Precision.HIGHEST, preferred_element_type=jnp.float32)
    hidden_cond = residual[0].astype(jnp.float32) + gate_row * jnp.dot(attn[0], out_weight, preferred_element_type=jnp.float32)
    hidden_uncond = residual[1].astype(jnp.float32) + gate_row * jnp.dot(attn[1], out_weight, preferred_element_type=jnp.float32)
    guided = hidden_uncond + 5.0 * (hidden_cond - hidden_uncond)
    return guided.astype(jnp.bfloat16)
```

```python
import functools
import math

import jax
import jax.numpy as jnp
from jax import lax
from jax.experimental import pallas as pl
from jax.experimental.pallas import tpu as pltpu
from jax.sharding import PartitionSpec as P

HEAD_DIM = 128
GUIDE_SCALE = 5.0
SCORE_SCALE = 1.0 / math.sqrt(HEAD_DIM)
EXP_SCALE = SCORE_SCALE / math.log(2.0)


def rotation_tables(positions):
    half_dim = HEAD_DIM // 2
    side_pairs = HEAD_DIM // 6
    frame_pairs = half_dim - 2 * side_pairs
    lane = lax.iota(jnp.int32, HEAD_DIM)
    pair_index = lane // 2
    section = (pair_index >= frame_pairs).astype(jnp.int32) + (
        pair_index >= frame_pairs + side_pairs
    ).astype(jnp.int32)
    local_index = pair_index - jnp.where(
        section == 0, 0, jnp.where(section == 1, frame_pairs, frame_pairs + side_pairs)
    )
    section_pairs = jnp.where(section == 0, frame_pairs, side_pairs)
    exponent = local_index.astype(jnp.float32) / section_pairs.astype(jnp.float32)
    freqs = jnp.power(jnp.float32(10000.0), -exponent)
    place = positions.astype(jnp.float32)
    chosen = jnp.where(
        section[None, :] == 0,
        place[0][:, None],
        jnp.where(section[None, :] == 1, place[1][:, None], place[2][:, None]),
    )
    angles = chosen * freqs[None, :]
    sign = jnp.where(lane % 2 == 0, -1.0, 1.0).astype(jnp.float32)
    return jnp.cos(angles), jnp.sin(angles) * sign[None, :]


def split_kernel(side, key_in, value_in, give, keep):
    width = give.shape[2]
    for refs, side_now in ((give, 1 - side[0]), (keep, side[0])):
        for half in range(2):

            @pl.when(side_now == half)
            def _():
                refs[0] = key_in[:, half * width : (half + 1) * width]
                refs[1] = value_in[:, half * width : (half + 1) * width]


def split_stale(side, keys, values):
    tok_rows, width = keys.shape
    out = jax.ShapeDtypeStruct((2, tok_rows, width // 2), keys.dtype)
    return pl.pallas_call(
        split_kernel,
        out_shape=(out, out),
        in_specs=[
            pl.BlockSpec(memory_space=pltpu.SMEM),
            pl.BlockSpec(memory_space=pltpu.VMEM),
            pl.BlockSpec(memory_space=pltpu.VMEM),
        ],
        name="split_stale",
    )(side, keys, values)


def turn(values, cosines, sines, even):
    wide = values.astype(jnp.float32)
    swapped = jnp.where(even, pltpu.roll(wide, HEAD_DIM - 1, 1), pltpu.roll(wide, 1, 1))
    return (wide * cosines + swapped * sines).astype(jnp.bfloat16)


def rotate_kernel(side, query_in, key_in, value_in, cos_ref, sin_ref, q_give, q_keep, f_give, f_keep):
    width = q_give.shape[1]
    cosines = cos_ref[...]
    sines = sin_ref[...]
    even = lax.broadcasted_iota(jnp.int32, cosines.shape, 1) % 2 == 0
    for half in range(2):
        base = half * width

        def fill(q_out, f_out):
            for at in range(0, width, HEAD_DIM):
                there = slice(at, at + HEAD_DIM)
                here = slice(base + at, base + at + HEAD_DIM)
                q_out[:, there] = turn(query_in[:, here], cosines, sines, even)
                f_out[0, :, there] = turn(key_in[:, here], cosines, sines, even)
                f_out[1, :, there] = value_in[:, here]

        @pl.when(side[0] == half)
        def _():
            fill(q_keep, f_keep)

        @pl.when(side[0] != half)
        def _():
            fill(q_give, f_give)


def rotate_fresh(side, queries, keys, values, cosines, sines):
    tok_rows, width = queries.shape
    one = jax.ShapeDtypeStruct((tok_rows, width // 2), jnp.bfloat16)
    two = jax.ShapeDtypeStruct((2, tok_rows, width // 2), jnp.bfloat16)
    return pl.pallas_call(
        rotate_kernel,
        out_shape=(one, one, two, two),
        in_specs=[pl.BlockSpec(memory_space=pltpu.SMEM)]
        + [pl.BlockSpec(memory_space=pltpu.VMEM)] * 5,
        name="rotate_fresh",
    )(side, queries, keys, values, cosines, sines)


def pick_lane(stats, lane_ids, lane):
    return jnp.sum(jnp.where(lane_ids == lane, stats, 0.0), axis=1, keepdims=True)


def attend_kernel(n_pieces, carried, final, send_stats, *refs):
    refs = list(refs)
    query = refs.pop(0)
    pieces = [refs.pop(0) for _ in range(n_pieces)]
    if carried:
        acc_in, top_in, total_in = refs.pop(0), refs.pop(0), refs.pop(0)
    tok_rows, width = query.shape
    lane_ids = lax.broadcasted_iota(jnp.int32, (tok_rows, HEAD_DIM), 1)
    stat_a = jnp.zeros((tok_rows, HEAD_DIM), jnp.float32)
    stat_b = jnp.zeros((tok_rows, HEAD_DIM), jnp.float32)
    for head in range(width // HEAD_DIM):
        cols = slice(head * HEAD_DIM, (head + 1) * HEAD_DIM)
        keys = jnp.concatenate([piece[0, :, cols] for piece in pieces], axis=0)
        values = jnp.concatenate([piece[1, :, cols] for piece in pieces], axis=0)
        scores = lax.dot_general(
            query[:, cols], keys, (((1,), (1,)), ((), ())), preferred_element_type=jnp.float32
        )
        top = jnp.max(scores, axis=1, keepdims=True)
        if carried:
            top_old = pick_lane(top_in[...], lane_ids, head)
            top = jnp.maximum(top, top_old)
        expo = jnp.exp2((scores - top) * EXP_SCALE)
        total = jnp.sum(expo, axis=1, keepdims=True)
        summed = jnp.dot(expo.astype(jnp.bfloat16), values, preferred_element_type=jnp.float32)
        if carried:
            fade = jnp.exp2((top_old - top) * EXP_SCALE)
            total = total + fade * pick_lane(total_in[...], lane_ids, head)
            summed = summed + fade * acc_in[:, cols]
        if final:
            refs[0][:, cols] = (summed / total).astype(jnp.bfloat16)
            if send_stats:
                stat_a = jnp.where(lane_ids == head, top * EXP_SCALE + jnp.log2(total), stat_a)
        else:
            refs[0][:, cols] = summed
            stat_a = jnp.where(lane_ids == head, top, stat_a)
            stat_b = jnp.where(lane_ids == head, total, stat_b)
    if not final:
        refs[1][...] = stat_a
        refs[2][...] = stat_b
    elif send_stats:
        refs[1][...] = stat_a.T[: refs[1].shape[0]]


def attend(query, pieces, carry=None, final=False, send_stats=False, name="attend"):
    tok_rows, width = query.shape
    stat = jax.ShapeDtypeStruct((tok_rows, HEAD_DIM), jnp.float32)
    if final:
        outs = [jax.ShapeDtypeStruct((tok_rows, width), jnp.bfloat16)]
        if send_stats:
            lines = -(-(width // HEAD_DIM) // 8) * 8
            outs.append(jax.ShapeDtypeStruct((lines, tok_rows), jnp.float32))
    else:
        outs = [jax.ShapeDtypeStruct((tok_rows, width), jnp.float32), stat, stat]
    operands = [query, *pieces] + (list(carry) if carry is not None else [])
    return pl.pallas_call(
        functools.partial(attend_kernel, len(pieces), carry is not None, final, send_stats),
        out_shape=outs,
        in_specs=[pl.BlockSpec(memory_space=pltpu.VMEM)] * len(operands),
        out_specs=[pl.BlockSpec(memory_space=pltpu.VMEM)] * len(outs),
        name=name,
    )(*operands)


def merge_kernel(far, far_stat, acc, top, total, out):
    tok_rows, width = out.shape
    lane_ids = lax.broadcasted_iota(jnp.int32, (tok_rows, HEAD_DIM), 1)
    pad = jnp.zeros((HEAD_DIM - far_stat.shape[0], tok_rows), jnp.float32)
    far_log = jnp.concatenate([far_stat[...], pad], axis=0).T
    peak = jnp.maximum(far_log, top[...] * EXP_SCALE)
    weight_far = jnp.exp2(far_log - peak)
    weight_own = jnp.exp2(top[...] * EXP_SCALE - peak)
    scale = 1.0 / (weight_far + weight_own * total[...])
    weight_far = weight_far * scale
    weight_own = weight_own * scale
    for head in range(width // HEAD_DIM):
        cols = slice(head * HEAD_DIM, (head + 1) * HEAD_DIM)
        out[:, cols] = (
            far[:, cols].astype(jnp.float32) * pick_lane(weight_far, lane_ids, head)
            + acc[:, cols] * pick_lane(weight_own, lane_ids, head)
        ).astype(jnp.bfloat16)


def merge(far, far_stat, carry):
    return pl.pallas_call(merge_kernel, out_shape=far, name="merge")(far, far_stat, *carry)


def project_kernel(with_rest, index, mix, keep_a, keep_b, give_a, give_b, w_keep, w_give, gate, *refs):
    refs = list(refs)
    rest = [refs.pop(0), refs.pop(0)] if with_rest else None
    out, c_keep, c_give = refs

    @pl.when(pl.program_id(0) == 0)
    def _():
        for scratch, mine, other in ((c_keep, keep_a, keep_b), (c_give, give_a, give_b)):
            scratch[...] = (
                mix[0] * mine[...].astype(jnp.float32) + mix[1] * other[...].astype(jnp.float32)
            ).astype(jnp.bfloat16)

    proj = jnp.dot(c_keep[...], w_keep[...], preferred_element_type=jnp.float32) + jnp.dot(
        c_give[...], w_give[...], preferred_element_type=jnp.float32
    )
    proj = proj * gate[...]
    if with_rest:
        proj = proj + (
            mix[0] * rest[0][...].astype(jnp.float32) + mix[1] * rest[1][...].astype(jnp.float32)
        )
    out[...] = proj.astype(out.dtype)


def project(index, mix, parts, weight, gate, out_width, dtype, rest=None, name="project"):
    tok_rows, half = parts[0].shape
    block = 256 if out_width % 256 == 0 else HEAD_DIM
    steps = out_width // block
    whole = pl.BlockSpec((tok_rows, half), lambda j, index, mix: (0, 0))
    in_specs = [whole] * 4 + [
        pl.BlockSpec((half, block), lambda j, index, mix: (index[0], index[1] * steps + j)),
        pl.BlockSpec((half, block), lambda j, index, mix: (1 - index[0], index[1] * steps + j)),
        pl.BlockSpec((1, block), lambda j, index, mix: (0, index[1] * steps + j)),
    ]
    operands = [*parts, weight, weight, gate]
    if rest is not None:
        in_specs += [
            pl.BlockSpec((tok_rows, block), lambda j, index, mix: (0, index[2] * steps + j)),
            pl.BlockSpec((tok_rows, block), lambda j, index, mix: (0, j)),
        ]
        operands += rest
    return pl.pallas_call(
        functools.partial(project_kernel, rest is not None),
        out_shape=jax.ShapeDtypeStruct((tok_rows, out_width), dtype),
        grid_spec=pltpu.PrefetchScalarGridSpec(
            num_scalar_prefetch=2,
            grid=(steps,),
            in_specs=in_specs,
            out_specs=pl.BlockSpec((tok_rows, block), lambda j, index, mix: (0, j)),
            scratch_shapes=[pltpu.VMEM((tok_rows, half), jnp.bfloat16)] * 2,
        ),
        name=name,
    )(index, mix, *operands)


def flip(value, axis, size, bit=0):
    return lax.ppermute(value, axis, [(at, at ^ (1 << bit)) for at in range(size)])


def per_device(
    patch_size,
    fresh_q,
    fresh_k,
    fresh_v,
    stale_k,
    stale_v,
    positions,
    residual,
    out_weight,
    gate_table,
    timestep,
):
    far_bits = range(2, patch_size.bit_length() - 1)
    patch_flip = functools.partial(flip, axis="patch", size=patch_size)
    guide = lax.axis_index("guide")
    tensor = lax.axis_index("tensor")
    side = (lax.axis_index("patch") // 2) % 2
    side_ref = side.astype(jnp.int32)[None]

    give, keep = split_stale(side_ref, stale_k[0], stale_v[0])
    crossed = patch_flip(give, bit=1)
    near = [keep]
    late = [crossed]
    for bit in far_bits:
        near = near + [patch_flip(piece, bit=bit) for piece in near]
        late = late + [patch_flip(piece, bit=bit) for piece in late]
    near = near + [patch_flip(piece, bit=0) for piece in near]
    late = late + [patch_flip(piece, bit=0) for piece in late]
    half_late = len(late) // 2

    cosines, sines = rotation_tables(positions)
    q_give, q_keep, f_give, f_keep = rotate_fresh(
        side_ref, fresh_q[0], fresh_k[0], fresh_v[0], cosines, sines
    )
    q_far = patch_flip(q_give, bit=1)
    quarter = residual.shape[2] // 2
    rest_other = flip(
        lax.dynamic_slice_in_dim(residual[0], (1 - guide) * quarter, quarter, 1), "guide", 2
    )

    own_part = attend(q_give, [f_give], name="attend_own")
    first_late = [late[half_late]]
    last_late = [piece for at, piece in enumerate(late) if at not in (0, half_late)]
    carry_far = attend(q_far, near + first_late, name="attend_far_1")
    carry_keep = attend(q_keep, [f_keep] + near[1:] + [late[0]] + first_late, name="attend_keep_1")
    o_far, far_stat = attend(
        q_far, last_late, carry_far, final=True, send_stats=True, name="attend_far_2"
    )
    (a_keep,) = attend(q_keep, last_late, carry_keep, final=True, name="attend_keep_2")
    back_stat = patch_flip(far_stat, bit=1)
    back = patch_flip(o_far, bit=1)
    b_keep = flip(a_keep, "guide", 2)
    a_give = merge(back, back_stat, own_part)
    b_give = flip(a_give, "guide", 2)

    gate_row = lax.dynamic_slice_in_dim(gate_table, timestep[0], 1, 0)
    mix = jnp.where(
        guide == 0,
        jnp.array([GUIDE_SCALE, 1.0 - GUIDE_SCALE], jnp.float32),
        jnp.array([1.0 - GUIDE_SCALE, GUIDE_SCALE], jnp.float32),
    )
    parts = [a_keep, b_keep, a_give, b_give]
    index_out = jnp.stack([side, (1 - tensor) * 2 + guide, guide]).astype(jnp.int32)
    index_own = jnp.stack([side, tensor * 2 + guide, guide]).astype(jnp.int32)
    send = project(
        index_out, mix, parts, out_weight, gate_row, quarter, jnp.bfloat16, name="project_out"
    )
    arrived = flip(send, "tensor", 2)
    own = project(
        index_own,
        mix,
        parts,
        out_weight,
        gate_row,
        quarter,
        jnp.float32,
        rest=[residual[0], rest_other],
        name="project_own",
    )
    return (own + arrived.astype(jnp.float32)).astype(jnp.bfloat16)


def solution(mesh):
    in_specs = (
        P("guide", "patch", "tensor"),
        P("guide", "patch", "tensor"),
        P("guide", "patch", "tensor"),
        P("guide", "patch", "tensor"),
        P("guide", "patch", "tensor"),
        P(None, "patch"),
        P("guide", "patch", "tensor"),
        P("tensor", None),
        P(),
        P(),
    )
    out_specs = P("patch", ("tensor", "guide"))
    return jax.shard_map(
        functools.partial(per_device, mesh.shape["patch"]),
        mesh=mesh,
        in_specs=in_specs,
        out_specs=out_specs,
        check_vma=False,
    )
```
